32 devices in a mesh: rep: 4 (over y, core), shard: 8 (over z, x).
Axes of the slice: x: 2, y: 2, z: 4, core: 2. Of those that a mesh axis runs over, the one named last changes fastest.
Arguments:
- tokens: bfloat16 [32768, 1024], P(('rep', 'shard')), may hold values from -6 to 6
- cotangent: bfloat16 [32768, 1024], P(('rep', 'shard')), may hold values from -6 to 6
- deal_source: int32 [4, 64], P('rep'), may hold values from 0 to 63, as said below
- deal_first: int32 [4, 64], P('rep'), may hold values from 0 to 7, as said below
- deal_length: int32 [4, 64], P('rep'), may hold values from 1 to 1024, as said below
- qkv_weight: bfloat16 [1024, 3072], P('shard'), may hold values from -0.1875 to 0.1875
- query_bias: bfloat16 [1024], P('shard'), may hold values from -3 to 3
- value_bias: bfloat16 [1024], P('shard'), may hold values from -3 to 3
- out_weight: bfloat16 [1024, 1024], P('shard'), may hold values from -0.5 to 0.5
- out_bias: bfloat16 [1024], P('shard'), may hold values from -3 to 3
- first_gain: bfloat16 [1024], P('shard'), may hold values from 0.25 to 1.75
- first_shift: bfloat16 [1024], P('shard'), may hold values from -2 to 2
- up_weight: bfloat16 [1024, 4096], P('shard'), may hold values from -0.1875 to 0.1875
- up_bias: bfloat16 [4096], P('shard'), may hold values from -3 to 3
- down_weight: bfloat16 [4096, 1024], P('shard'), may hold values from -0.09375 to 0.09375
- down_bias: bfloat16 [1024], P('shard'), may hold values from -3 to 3
- second_gain: bfloat16 [1024], P('shard'), may hold values from 0.25 to 1.75
- second_shift: bfloat16 [1024], P('shard'), may hold values from -2 to 2
Outputs:
- output: bfloat16 [32768, 1024], P(('rep', 'shard'))
- input_grad: bfloat16 [32768, 1024], P(('rep', 'shard'))
- qkv_weight_grad: float32 [1024, 3072], P('shard')
- query_bias_grad: float32 [1024], P('shard')
- value_bias_grad: float32 [1024], P('shard')
- out_weight_grad: float32 [1024, 1024], P('shard')
- out_bias_grad: float32 [1024], P('shard')
- first_gain_grad: float32 [1024], P('shard')
- first_shift_grad: float32 [1024], P('shard')
- up_weight_grad: float32 [1024, 4096], P('shard')
- up_bias_grad: float32 [4096], P('shard')
- down_weight_grad: float32 [4096, 1024], P('shard')
- down_bias_grad: float32 [1024], P('shard')
- second_gain_grad: float32 [1024], P('shard')
- second_shift_grad: float32 [1024], P('shard')
The draws below stay inside these ranges and needn't reach their ends.
Inputs may be any that keep to these rules, and one draw needn't show every extreme that they name: `deal_source`: in each group, a permutation of the group's blocks; every sequence's blocks are consecutive and in order both in the given order and in the dealt order, and all lie on one device. `deal_first`: equal for all blocks of one sequence, and equal to the block's own local index at a sequence's first block. `deal_length`: equal for all blocks of one sequence; a sequence of n blocks has a length above (n - 1) * 128.
All inputs are finite; a program needn't handle non-finite values.
Results may differ from the reference program's by a relative error of at most 0.019.
Values may be sent and summed in bfloat16 or wider, within the bound.
No kernel may reach another device: no remote copies, remote signals or barrier semaphores. Data moves between devices by JAX's collectives and lax.ppermute only.
A program may use at most 320 MiB of HBM per device.

```python
import jax
import jax.numpy as jnp
from jax import lax

D = 1024
HDIM = 64
FF = 4096
TOK_DEV = 1024
BLOCK = 128
BLOCKS_DEV = 8
SLOTS = 64
TOKENS = 32768
N_REP = 4
N_SHARD = 8


def deal_tables(key):
    block_count = TOK_DEV // BLOCK
    slot_total = block_count * N_SHARD
    base_key = jax.random.fold_in(key, 4021)
    cut_key, padding_key, order_key = jax.random.split(base_key, 3)
    slot_index = jnp.arange(slot_total, dtype=jnp.int32)
    local_slot = slot_index % block_count
    cut_flags = jax.random.randint(cut_key, (N_REP, slot_total), 0, 2)
    forced_cut = slot_index == 2 * block_count - 1
    later_device = slot_index >= block_count
    starts = (local_slot == 0)[None, :] | (cut_flags == 1) & later_device[None, :] | forced_cut[None, :]
    first_slot = lax.cummax(jnp.where(starts, slot_index[None, :], 0), axis=1)
    block_counts = jnp.sum((first_slot[:, None, :] == slot_index[None, :, None]).astype(jnp.int32), axis=2)
    padding = jax.random.randint(padding_key, (N_REP, slot_total), 0, BLOCK)
    padding = jnp.where(later_device[None, :], padding, 0)
    padding = jnp.where(forced_cut[None, :], BLOCK - 1, padding)
    start_length = block_counts * BLOCK - padding
    lengths = jnp.take_along_axis(start_length, first_slot, axis=1)
    order_score = jax.random.randint(order_key, (N_REP, slot_total), 0, slot_total) * slot_total + slot_index[None, :]
    earlier = starts[:, None, :] & (order_score[:, None, :] < order_score[:, :, None])
    offsets = jnp.sum(jnp.where(earlier, block_counts[:, None, :], 0), axis=2)
    sources = jnp.take_along_axis(offsets, first_slot, axis=1) + slot_index[None, :] - first_slot
    return (sources.astype(jnp.int32), (first_slot % block_count).astype(jnp.int32), lengths.astype(jnp.int32))


def draw_deal_source(key, part):
    return deal_tables(key)[0]


def draw_deal_first(key, part):
    return deal_tables(key)[1]


def draw_deal_length(key, part):
    return deal_tables(key)[2]


def level_of(rng, dims, cuts, low, largest):
    def one(dim, shards_of):
        draws = jax.random.uniform(jax.random.fold_in(jax.random.fold_in(rng, 6), dim), (shards_of,), jnp.float32, low / len(cuts), largest / len(cuts))
        return jnp.repeat(jnp.exp(draws), dims[dim] // shards_of).reshape((-1,) + (1,) * (len(dims) - dim - 1))

    level = one(*cuts[0])
    for cut in cuts[1:]:
        level = level * one(*cut)
    return level


def noise(own_key, shape, deviation, reach, shards=(), kind=jnp.bfloat16):
    entries = jax.random.normal(own_key, shape, jnp.float32) * deviation
    if len(shards) > 0:
        entries = level_of(own_key, shape, shards, -0.22, 0.18) * entries
    return jnp.clip(entries, min=-reach, max=reach).astype(kind)


def setup_inputs(seed: int = 0) -> dict:
    key_of = jax.random.split(jax.random.key(seed), 19)
    return {
        "tokens": noise(key_of[0], (TOKENS, D), 1.0, 6.0, ((0, 32),)),
        "cotangent": noise(key_of[1], (TOKENS, D), 1.0, 6.0, ((0, 32),)),
        "deal_source": draw_deal_source(jax.random.fold_in(key_of[18], 71), 0),
        "deal_first": draw_deal_first(jax.random.fold_in(key_of[18], 71), 0),
        "deal_length": draw_deal_length(jax.random.fold_in(key_of[18], 71), 0),
        "qkv_weight": noise(key_of[5], (D, 3 * D), D ** -0.5, 0.1875, ((0, 8),)),
        "query_bias": noise(key_of[6], (D,), 0.5, 3.0, ((0, 8),)),
        "value_bias": noise(key_of[7], (D,), 0.5, 3.0, ((0, 8),)),
        "out_weight": noise(key_of[8], (D, D), (D // 8) ** -0.5, 0.5, ((0, 8),)),
        "out_bias": noise(key_of[9], (D,), 0.5, 3.0, ((0, 8),)),
        "first_gain": jnp.clip(1.0 + 0.15 * jax.random.normal(key_of[10], (D,), jnp.float32), 0.25, 1.75).astype(jnp.bfloat16),
        "first_shift": noise(key_of[11], (D,), 0.3, 2.0, ((0, 8),)),
        "up_weight": noise(key_of[12], (D, FF), D ** -0.5, 0.1875, ((0, 8),)),
        "up_bias": noise(key_of[13], (FF,), 0.5, 3.0, ((0, 8),)),
        "down_weight": noise(key_of[14], (FF, D), FF ** -0.5, 0.09375, ((0, 8),)),
        "down_bias": noise(key_of[15], (D,), 0.5, 3.0, ((0, 8),)),
        "second_gain": jnp.clip(1.0 + 0.15 * jax.random.normal(key_of[16], (D,), jnp.float32), 0.25, 1.75).astype(jnp.bfloat16),
        "second_shift": noise(key_of[17], (D,), 0.3, 2.0, ((0, 8),)),
    }


NORM_EPSILON = 1e-05

@jax.custom_vjp
def low(v):
    return lax.optimization_barrier(v.astype(jnp.bfloat16)).astype(jnp.float32)

@jax.custom_vjp
def low_back(v):
    return v

def low_keep(v):
    return (low(v), None)

def low_pass(kept, grad):
    return (grad,)

def back_keep(v):
    return (v, None)

def back_low(kept, grad):
    return (low(grad),)
low.defvjp(low_keep, low_pass)
low_back.defvjp(back_keep, back_low)

def layer_norm(resid, gain, shift):
    row_mean = lax.optimization_barrier(jnp.mean(resid, axis=-1, keepdims=True))
    centred = resid - row_mean
    variance = lax.optimization_barrier(jnp.mean(centred * centred, axis=-1, keepdims=True))
    return centred * lax.rsqrt(variance + NORM_EPSILON) * gain + shift

def gelu_exact(tensor):
    return 0.5 * tensor * (1.0 + lax.erf(tensor * 0.7071067811865476))

def forward(inputs, qkv_weight, query_bias, value_bias, out_weight, out_bias, first_gain, first_shift, up_weight, up_bias, down_weight, down_bias, second_gain, second_shift, allowed):
    highest = lax.Precision.HIGHEST
    row_count, feature_width = inputs.shape
    head_count = feature_width // HDIM
    qkv_bias = jnp.concatenate([query_bias, jnp.zeros_like(query_bias), value_bias])
    qkv_rows = low_back(low(jnp.dot(inputs, qkv_weight, precision=highest) + qkv_bias))
    head_shape = (row_count, head_count, HDIM)
    queries = qkv_rows[:, :feature_width].reshape(head_shape)
    key_part = qkv_rows[:, feature_width:2 * feature_width].reshape(head_shape)
    values = qkv_rows[:, 2 * feature_width:].reshape(head_shape)
    scores = low_back(jnp.einsum('qhd,khd->hqk', queries, key_part, precision=highest) * HDIM ** (-0.5))
    scores = jnp.where(allowed[None], scores, -1e+30)
    row_max = lax.optimization_barrier(jnp.max(scores, axis=-1, keepdims=True))
    exponent = jnp.exp(scores - row_max)
    weights = low(exponent / lax.optimization_barrier(jnp.sum(exponent, axis=-1, keepdims=True)))
    mixed_rows = jnp.einsum('hqk,khd->qhd', weights, values, precision=highest).reshape(row_count, feature_width)
    mixed_rows = low_back(low(mixed_rows))
    branch = low_back(jnp.dot(mixed_rows, out_weight, precision=highest) + out_bias)
    normed = layer_norm(inputs + branch, first_gain, first_shift)
    gate_value = low_back(jnp.dot(low(normed), up_weight, precision=highest) + up_bias)
    hidden = low(gelu_exact(gate_value))
    second = low_back(jnp.dot(hidden, down_weight, precision=highest) + down_bias)
    return layer_norm(normed + second, second_gain, second_shift)

def reference(tokens, cotangent, deal_source, deal_first, deal_length, qkv_weight, query_bias, value_bias, out_weight, out_bias, first_gain, first_shift, up_weight, up_bias, down_weight, down_bias, second_gain, second_shift):
    unit_total = N_REP * N_SHARD
    group_rows = jnp.arange(N_REP, dtype=jnp.int32)[:, None]
    sources = deal_source.astype(jnp.int32)

    def to_dealt(tensor):
        blocked = tensor.astype(jnp.float32).reshape(N_REP, SLOTS, BLOCK, D)
        return blocked[group_rows, sources].reshape(unit_total, TOK_DEV, D)
    dealt_inputs = to_dealt(tokens)
    dealt_grads = to_dealt(cotangent)
    firsts = deal_first.reshape(unit_total, BLOCKS_DEV)
    lengths = deal_length.reshape(unit_total, BLOCKS_DEV)
    params = tuple((tensor.astype(jnp.float32) for tensor in (qkv_weight, query_bias, value_bias, out_weight, out_bias, first_gain, first_shift, up_weight, up_bias, down_weight, down_bias, second_gain, second_shift)))

    def unit_step(running, item):
        unit_inputs, unit_grads, unit_firsts, unit_lengths = item
        row_first = jnp.repeat(unit_firsts, BLOCK, total_repeat_length=TOK_DEV)
        row_length = jnp.repeat(unit_lengths, BLOCK, total_repeat_length=TOK_DEV)
        position = jnp.arange(TOK_DEV, dtype=jnp.int32) - row_first * BLOCK
        allowed = (row_first[:, None] == row_first[None, :]) & (position < row_length)[None, :]

        def layer(layer_inputs, *weight_list):
            return forward(layer_inputs, *weight_list, allowed)
        layer_out, pull_back = jax.vjp(layer, unit_inputs, *params)
        grads = pull_back(unit_grads)
        running = tuple((left_sum + right_grad for left_sum, right_grad in zip(running, grads[1:])))
        return (running, (layer_out, grads[0]))
    zero_sums = tuple((jnp.zeros(tensor.shape, jnp.float32) for tensor in params))
    sums, (outputs, backs) = lax.scan(unit_step, zero_sums, (dealt_inputs, dealt_grads, firsts, lengths))

    def to_given(tensor):
        blocked = tensor.reshape(N_REP, SLOTS, BLOCK, D)
        return jnp.zeros_like(blocked).at[group_rows, sources].set(blocked).reshape(N_REP * SLOTS * BLOCK, D)
    return (to_given(outputs).astype(jnp.bfloat16), to_given(backs).astype(jnp.bfloat16), sums[0], sums[1], sums[2], sums[3], sums[4], sums[5], sums[6], sums[7], sums[8], sums[9], sums[10], sums[11], sums[12])
```

```python
import functools

import jax
import jax.numpy as jnp
from jax import lax
from jax.experimental import pallas as pl
from jax.experimental.pallas import tpu as pltpu
from jax.sharding import PartitionSpec as P

HDIM = 64
BLOCK = 128
PAIR = 2 * HDIM
NORM_EPSILON = 1e-05
NEGATIVE = -1e30


def layer_norm(resid, gain, shift):
    row_mean = jnp.mean(resid, axis=-1, keepdims=True)
    centred = resid - row_mean
    variance = jnp.mean(centred * centred, axis=-1, keepdims=True)
    return centred * lax.rsqrt(variance + NORM_EPSILON) * gain + shift


def gelu_exact(tensor):
    return 0.5 * tensor * (1.0 + lax.erf(tensor * 0.7071067811865476))


def contract_last(left_side, right_side):
    return lax.dot_general(
        left_side, right_side, (((1,), (1,)), ((), ())), preferred_element_type=jnp.float32
    )


def contract_rows(left_side, right_side):
    return lax.dot_general(
        left_side, right_side, (((0,), (0,)), ((), ())), preferred_element_type=jnp.float32
    )


def matmul(left_side, right_side):
    return jnp.dot(left_side, right_side, preferred_element_type=jnp.float32)


def sizes_of(block_count):
    sizes = [1]
    while sizes[-1] < block_count:
        sizes.append(min(2 * sizes[-1], block_count))
    return sizes


def by_size(length, block_count, body):
    sizes = sizes_of(block_count)
    for index, size in enumerate(sizes):
        fits = length <= size * BLOCK
        if index > 0:
            fits = fits & (length > sizes[index - 1] * BLOCK)
        pl.when(fits)(functools.partial(body, size * BLOCK))


def stack_heads(rows):
    lane = lax.broadcasted_iota(jnp.int32, rows.shape, 1)
    zero = jnp.zeros_like(rows)
    return jnp.concatenate(
        [jnp.where(lane < HDIM, rows, zero), jnp.where(lane >= HDIM, rows, zero)], axis=0
    )


def forward_kernel(info, qkv, out, *, halo, block_count):
    def one_block(index, carry):
        first = info[0, halo + index]
        length = info[1, halo + index]
        row = pl.multiple_of((halo + index) * BLOCK, BLOCK)

        def body(size):
            start = pl.multiple_of(first * BLOCK, BLOCK)
            queries = stack_heads(qkv[pl.ds(row, BLOCK), :PAIR] * jnp.bfloat16(HDIM ** (-0.5)))
            keys = qkv[pl.ds(start, size), PAIR : 2 * PAIR]
            values = qkv[pl.ds(start, size), 2 * PAIR :]
            scores = contract_last(queries, keys)
            column = lax.broadcasted_iota(jnp.int32, scores.shape, 1)
            scores = jnp.where(column < length, scores, NEGATIVE)
            exponent = jnp.exp(scores - jnp.max(scores, axis=1, keepdims=True))
            total = jnp.sum(exponent, axis=1, keepdims=True)
            mixed = matmul(exponent.astype(jnp.bfloat16), values) / total
            lane = lax.broadcasted_iota(jnp.int32, (BLOCK, PAIR), 1)
            out[pl.ds(pl.multiple_of(index * BLOCK, BLOCK), BLOCK), :] = jnp.where(
                lane < HDIM, mixed[:BLOCK], mixed[BLOCK:]
            ).astype(jnp.bfloat16)

        by_size(length, block_count, body)
        return carry

    lax.fori_loop(0, block_count, one_block, 0)


def backward_kernel(info, qkv, mixed_grad, out, key_turned, key_sum, value_sum, *, halo, block_count):
    key_turned[...] = qkv[:, PAIR : 2 * PAIR].astype(jnp.float32).T.astype(jnp.bfloat16)
    key_sum[...] = jnp.zeros_like(key_sum)
    value_sum[...] = jnp.zeros_like(value_sum)

    def one_block(index, carry):
        first = info[0, index]
        length = info[1, index]
        row = pl.multiple_of(index * BLOCK, BLOCK)

        def body(size):
            start = pl.multiple_of(first * BLOCK, BLOCK)
            queries = stack_heads(qkv[pl.ds(row, BLOCK), :PAIR] * jnp.bfloat16(HDIM ** (-0.5)))
            grads = stack_heads(mixed_grad[pl.ds(row, BLOCK), :])
            keys = qkv[pl.ds(start, size), PAIR : 2 * PAIR]
            values = qkv[pl.ds(start, size), 2 * PAIR :]
            scores = contract_last(keys, queries)
            place = lax.broadcasted_iota(jnp.int32, scores.shape, 0)
            scores = jnp.where(place < length, scores, NEGATIVE)
            exponent = jnp.exp(scores - jnp.max(scores, axis=0, keepdims=True))
            weights = exponent * (1.0 / jnp.sum(exponent, axis=0, keepdims=True))
            value_sum[pl.ds(start, size), :] += matmul(weights.astype(jnp.bfloat16), grads)
            weight_grad = contract_last(values, grads)
            shared = jnp.sum(weights * weight_grad, axis=0, keepdims=True)
            score_grad = (weights * (weight_grad - shared)).astype(jnp.bfloat16)
            key_sum[pl.ds(start, size), :] += matmul(score_grad, queries)

            @pl.when((index >= halo) & (index < halo + block_count))
            def _():
                turned = matmul(key_turned[:, pl.ds(start, size)], score_grad)
                lane = lax.broadcasted_iota(jnp.int32, (PAIR, BLOCK), 0)
                query_grad = jnp.where(lane < HDIM, turned[:, :BLOCK], turned[:, BLOCK:]).T
                own = pl.multiple_of((index - halo) * BLOCK, BLOCK)
                out[pl.ds(own, BLOCK), :PAIR] = (query_grad * HDIM ** (-0.5)).astype(jnp.bfloat16)

        by_size(length, block_count, body)
        return carry

    lax.fori_loop(info[2, 0], info[2, 1], one_block, 0)
    own_rows = block_count * BLOCK
    out[:, PAIR : 2 * PAIR] = key_sum[halo * BLOCK : halo * BLOCK + own_rows, :].astype(jnp.bfloat16)
    out[:, 2 * PAIR :] = value_sum[halo * BLOCK : halo * BLOCK + own_rows, :].astype(jnp.bfloat16)


def attend(info, qkv_window, halo, block_count):
    window_rows, width = qkv_window.shape
    pairs = width // (3 * PAIR)
    own_rows = block_count * BLOCK
    return pl.pallas_call(
        functools.partial(forward_kernel, halo=halo, block_count=block_count),
        grid_spec=pltpu.PrefetchScalarGridSpec(
            num_scalar_prefetch=1,
            grid=(pairs,),
            in_specs=[pl.BlockSpec((window_rows, 3 * PAIR), lambda pair, info: (0, pair))],
            out_specs=pl.BlockSpec((own_rows, PAIR), lambda pair, info: (0, pair)),
        ),
        out_shape=jax.ShapeDtypeStruct((own_rows, pairs * PAIR), jnp.bfloat16),
        name="attend",
    )(info, qkv_window)


def attend_back(info, qkv_window, grad_window, halo, block_count):
    window_rows, width = qkv_window.shape
    pairs = width // (3 * PAIR)
    own_rows = block_count * BLOCK
    return pl.pallas_call(
        functools.partial(backward_kernel, halo=halo, block_count=block_count),
        grid_spec=pltpu.PrefetchScalarGridSpec(
            num_scalar_prefetch=1,
            grid=(pairs,),
            in_specs=[
                pl.BlockSpec((window_rows, 3 * PAIR), lambda pair, info: (0, pair)),
                pl.BlockSpec((window_rows, PAIR), lambda pair, info: (0, pair)),
            ],
            out_specs=pl.BlockSpec((own_rows, 3 * PAIR), lambda pair, info: (0, pair)),
            scratch_shapes=[
                pltpu.VMEM((PAIR, window_rows), jnp.bfloat16),
                pltpu.VMEM((window_rows, PAIR), jnp.float32),
                pltpu.VMEM((window_rows, PAIR), jnp.float32),
            ],
        ),
        out_shape=jax.ShapeDtypeStruct((own_rows, width), jnp.bfloat16),
        name="attend_back",
    )(info, qkv_window, grad_window)


def window_info(sources, firsts, lengths, shard, block_count, halo):
    slot_count = sources.shape[0]
    slots = jnp.arange(slot_count, dtype=jnp.int32)
    first_slot = slots // block_count * block_count + firsts
    first_given = jnp.sum(
        jnp.where(first_slot[:, None] == slots[None, :], sources[None, :], 0), axis=1
    )
    window = 2 * halo + block_count
    low = shard * block_count - halo
    given = low + jnp.arange(window, dtype=jnp.int32)
    here = sources[None, :] == given[:, None]
    start = jnp.sum(jnp.where(here, first_given[None, :], 0), axis=1) - low
    length = jnp.sum(jnp.where(here, lengths[None, :], 0), axis=1)
    last = start + (length + BLOCK - 1) // BLOCK
    begin = jnp.minimum(start[halo], halo)
    end = jnp.maximum(last[halo + block_count - 1], halo + block_count)
    bounds = jnp.where(jnp.arange(window) == 0, begin, jnp.where(jnp.arange(window) == 1, end, 0))
    return jnp.stack([start, length, bounds]).astype(jnp.int32)


def with_halo(rows, halo_rows, shard_count):
    up = [(index, index + 1) for index in range(shard_count - 1)]
    down = [(index + 1, index) for index in range(shard_count - 1)]
    left = lax.ppermute(rows[rows.shape[0] - halo_rows :], "shard", up)
    right = lax.ppermute(rows[:halo_rows], "shard", down)
    return jnp.concatenate([left, rows, right], axis=0)


def pack_small(parts, row_count):
    flat = jnp.concatenate(parts)
    width = -(-flat.shape[0] // (128 * row_count)) * 128
    return jnp.pad(flat, (0, row_count * width - flat.shape[0])).reshape(row_count, width)


def make_local(rep_count, shard_count):
    core_pairs = [(index, index ^ 1) for index in range(rep_count)]
    same_core = [list(range(core, rep_count, 2)) for core in range(2)]

    def sum_owned(summand, core):
        half = summand.shape[1] // 2
        own = lax.dynamic_slice_in_dim(summand, core * half, half, 1)
        other = lax.dynamic_slice_in_dim(summand, (1 - core) * half, half, 1)
        return own, lax.ppermute(other, "rep", core_pairs)

    def over_chips(part):
        if rep_count == 4:
            other = lax.ppermute(part, "rep", [(0, 2), (2, 0), (1, 3), (3, 1)])
            return part.astype(jnp.float32) + other.astype(jnp.float32)
        return lax.psum(part, "rep", axis_index_groups=same_core).astype(jnp.float32)

    def joined(part, core):
        mine = part.astype(jnp.bfloat16)
        other = lax.ppermute(mine, "rep", core_pairs)
        low = jnp.where(core == 0, mine, other)
        high = jnp.where(core == 0, other, mine)
        return jnp.concatenate([low, high], axis=1).astype(jnp.float32)

    def sum_weight(summand, core):
        own, other = sum_owned(summand.astype(jnp.bfloat16), core)
        both = (own.astype(jnp.float32) + other.astype(jnp.float32)).astype(jnp.bfloat16)
        part = lax.psum_scatter(both, "shard", scatter_dimension=0, tiled=True)
        return joined(over_chips(part), core)

    def local(
        tokens,
        cotangent,
        deal_source,
        deal_first,
        deal_length,
        qkv_weight,
        query_bias,
        value_bias,
        out_weight,
        out_bias,
        first_gain,
        first_shift,
        up_weight,
        up_bias,
        down_weight,
        down_bias,
        second_gain,
        second_shift,
    ):
        row_count, width = tokens.shape
        block_count = row_count // BLOCK
        halo = block_count - 1
        pairs = width // PAIR
        shard = lax.axis_index("shard")
        rep = lax.axis_index("rep")
        core = rep % 2
        info = window_info(deal_source[0], deal_first[0], deal_length[0], shard, block_count, halo)
        token_window = with_halo(tokens, halo * BLOCK, shard_count)

        held = qkv_weight.shape[0]
        share = held // rep_count
        hidden_width = up_weight.shape[1]
        grouped = (
            lax.dynamic_slice_in_dim(qkv_weight, rep * share, share, 0)
            .reshape(share, 3, pairs, PAIR)
            .swapaxes(1, 2)
            .reshape(share, 3 * width)
        )
        vectors = (
            query_bias,
            value_bias,
            out_bias,
            first_gain,
            first_shift,
            down_bias,
            second_gain,
            second_shift,
            up_bias,
        )
        lengths = [vector.shape[0] for vector in vectors]
        total = sum(lengths)
        packed = pack_small(vectors, share)
        first_block = jnp.concatenate(
            [grouped, lax.dynamic_slice_in_dim(out_weight, rep * share, share, 0), packed], axis=1
        )
        first_full = lax.all_gather(first_block, ("shard", "rep"), axis=0, tiled=True)
        full_qkv = first_full[:, : 3 * width]
        full_out = first_full[:, 3 * width : 4 * width]
        small = first_full[:, 4 * width :].reshape(shard_count, rep_count, -1)[:, 0, :total]
        small = small.astype(jnp.float32)
        pieces = []
        offset = 0
        for length in lengths:
            pieces.append(small[:, offset : offset + length].reshape(-1))
            offset += length
        (
            bias_query,
            bias_value,
            bias_out,
            gain_one,
            shift_one,
            bias_down,
            gain_two,
            shift_two,
            bias_up,
        ) = pieces
        full_up = lax.all_gather(
            lax.dynamic_slice_in_dim(up_weight, rep * share, share, 0),
            ("shard", "rep"),
            axis=0,
            tiled=True,
        )
        down_share = down_weight.shape[0] // rep_count
        full_down = lax.all_gather(
            lax.dynamic_slice_in_dim(down_weight, rep * down_share, down_share, 0),
            ("shard", "rep"),
            axis=0,
            tiled=True,
        )

        qkv_bias = jnp.stack(
            [
                bias_query.reshape(pairs, PAIR),
                jnp.zeros((pairs, PAIR), jnp.float32),
                bias_value.reshape(pairs, PAIR),
            ],
            axis=1,
        ).reshape(3 * width)
        qkv_window = (matmul(token_window, full_qkv) + qkv_bias).astype(jnp.bfloat16)
        mixed_rows = attend(info, qkv_window, halo, block_count)
        branch = matmul(mixed_rows, full_out) + bias_out
        normed, first_back = jax.vjp(
            layer_norm, tokens.astype(jnp.float32) + branch, gain_one, shift_one
        )
        normed_rows = normed.astype(jnp.bfloat16)

        gate_value = matmul(normed_rows, full_up) + bias_up
        hidden, gelu_back = jax.vjp(gelu_exact, gate_value)
        hidden_rows = hidden.astype(jnp.bfloat16)
        resid_two = normed + matmul(hidden_rows, full_down) + bias_down
        result, second_back = jax.vjp(layer_norm, resid_two, gain_two, shift_two)
        resid_two_grad, second_gain_grad, second_shift_grad = second_back(
            cotangent.astype(jnp.float32)
        )
        second_grad = resid_two_grad.astype(jnp.bfloat16)
        down_bias_grad = jnp.sum(second_grad.astype(jnp.float32), axis=0)
        down_grad = sum_weight(contract_rows(hidden_rows, second_grad), core)
        (gate_grad_full,) = gelu_back(contract_last(second_grad, full_down))
        gate_grad = gate_grad_full.astype(jnp.bfloat16)
        up_bias_grad = jnp.sum(gate_grad.astype(jnp.float32), axis=0)
        up_grad = sum_weight(contract_rows(normed_rows, gate_grad), core)
        normed_grad = resid_two_grad + contract_last(gate_grad, full_up)
        resid_one_grad, first_gain_grad, first_shift_grad = first_back(normed_grad)
        branch_grad = resid_one_grad.astype(jnp.bfloat16)
        out_bias_grad = jnp.sum(branch_grad.astype(jnp.float32), axis=0)
        out_grad = sum_weight(contract_rows(mixed_rows, branch_grad), core)

        mixed_grad = contract_last(branch_grad, full_out).astype(jnp.bfloat16)
        grad_window = with_halo(mixed_grad, halo * BLOCK, shard_count)
        qkv_grad = attend_back(info, qkv_window, grad_window, halo, block_count)
        input_grad = (resid_one_grad + contract_last(qkv_grad, full_qkv)).astype(jnp.bfloat16)
        bias_sums = jnp.sum(qkv_grad.astype(jnp.float32), axis=0).reshape(pairs, 3, PAIR)
        query_bias_grad = bias_sums[:, 0].reshape(width)
        value_bias_grad = bias_sums[:, 2].reshape(width)

        small_grads = (
            query_bias_grad,
            value_bias_grad,
            out_bias_grad,
            first_gain_grad,
            first_shift_grad,
            down_bias_grad,
            second_gain_grad,
            second_shift_grad,
            up_bias_grad,
        )
        flat = jnp.concatenate([piece.reshape(shard_count, -1) for piece in small_grads], axis=1)
        rows_each = -(-total // 128)
        extra = jnp.pad(flat, ((0, 0), (0, rows_each * 128 - total)))
        extra = extra.reshape(shard_count, rows_each, 128)
        extra = jnp.pad(extra, ((0, 0), (0, held - rows_each), (0, 0))).reshape(width, 128)
        extra = extra.astype(jnp.bfloat16)
        own, other = sum_owned(contract_rows(tokens, qkv_grad).astype(jnp.bfloat16), core)
        extra_other = lax.ppermute(extra, "rep", core_pairs)
        both = jnp.concatenate(
            [
                own.astype(jnp.float32) + other.astype(jnp.float32),
                extra.astype(jnp.float32) + extra_other.astype(jnp.float32),
            ],
            axis=1,
        ).astype(jnp.bfloat16)
        part = over_chips(lax.psum_scatter(both, "shard", scatter_dimension=0, tiled=True))
        half = both.shape[1] - 128
        qkv_owned = joined(part[:, :half], core)
        qkv_owned = (
            qkv_owned.reshape(held, pairs, 3, PAIR).swapaxes(1, 2).reshape(held, 3 * width)
        )
        owned_small = part[:rows_each, half:].reshape(-1)
        outs = []
        offset = 0
        for length in lengths:
            outs.append(owned_small[offset : offset + length])
            offset += length
        return (
            result.astype(jnp.bfloat16),
            input_grad,
            qkv_owned,
            outs[0],
            outs[1],
            out_grad,
            outs[2],
            outs[3],
            outs[4],
            up_grad,
            outs[8],
            down_grad,
            outs[5],
            outs[6],
            outs[7],
        )

    return local


def solution(mesh):
    return jax.shard_map(
        make_local(mesh.shape["rep"], mesh.shape["shard"]),
        mesh=mesh,
        in_specs=(
            P(("rep", "shard"), None),
            P(("rep", "shard"), None),
            P("rep", None),
            P("rep", None),
            P("rep", None),
            P("shard", None),
            P("shard"),
            P("shard"),
            P("shard", None),
            P("shard"),
            P("shard"),
            P("shard"),
            P("shard", None),
            P("shard"),
            P("shard", None),
            P("shard"),
            P("shard"),
            P("shard"),
        ),
        out_specs=(
            P(("rep", "shard"), None),
            P(("rep", "shard"), None),
            P("shard", None),
            P("shard"),
            P("shard"),
            P("shard", None),
            P("shard"),
            P("shard"),
            P("shard"),
            P("shard", None),
            P("shard"),
            P("shard", None),
            P("shard"),
            P("shard"),
            P("shard"),
        ),
        check_vma=False,
    )
```
